32 devices in a mesh: groups: 2 (over y), tm: 8 (over z, x), rows: 2 (over core).
Axes of the slice: x: 2, y: 2, z: 4, core: 2. Of those that a mesh axis runs over, the one named last changes fastest.
Arguments:
- states: bfloat16 [128, 4, 32, 512], P(('groups', 'tm'), 'rows'), parts along dimension 0, may hold values from -6 to 6
- inputs: bfloat16 [128, 4, 32, 256], P(('groups', 'tm'), 'rows'), parts along dimension 0, may hold values from -6 to 6
- grad_y: bfloat16 [128, 4, 32, 256], P(('groups', 'tm'), 'rows'), parts along dimension 0, may hold values from -0.59765625 to 0.59765625
- decay: float32 [128, 512], P(('groups', 'tm')), parts along dimension 0, may hold values from 0 to 1, as said below
- in_kernel: bfloat16 [2304, 512], P(('tm', 'rows')), may hold values from -0.125 to 0.125
- out_kernel: bfloat16 [4608, 256], P(('tm', 'rows')), may hold values from -0.09375 to 0.09375
Outputs:
- grad_inputs: bfloat16 [128, 4, 32, 256], P(('groups', 'tm'), 'rows'), parts along dimension 0
- grad_in_kernel: float32 [4608, 512], P(('groups', 'tm', 'rows')), parts along dimension 0
- grad_out_kernel: float32 [9216, 256], P(('groups', 'tm', 'rows')), parts along dimension 0
- grad_decay: float32 [128, 512], P(('groups', 'tm')), parts along dimension 0
The draws below stay inside these ranges and needn't reach their ends.
There are 2 independent parts, one for each index of `groups`. The reference program is written for one: setup_inputs(seed, part) draws one part's arguments, and reference() takes and returns one part's arrays. A program takes and returns all parts, laid end to end along the dimension named above; an argument that names none is the same for every part. Nothing has to cross between parts.
Inputs may be any that keep to these rules, and one draw needn't show every extreme that they name: `decay`: every entry lies strictly between 0 and 1.
All inputs are finite; a program needn't handle non-finite values.
Results may differ from the reference program's by a relative error of at most 0.0049.
Values may be sent and summed in bfloat16 or wider, within the bound.
A program may use at most 128 MiB of HBM per device.

```python
import jax
import jax.numpy as jnp
from jax import lax

P_SIZE = 512
U = 256
COLS = 32
SNAPSHOT_TOTAL = 64
H = 4


def draw_decay(key, part):
    stochastic_seeds = jax.random.split(jax.random.fold_in(key, 71), 6)
    slow_share = 0.5
    gradual_damping = jax.random.uniform(stochastic_seeds[0], (P_SIZE,), jnp.float32) < slow_share
    slow_rate = jnp.exp(jax.random.uniform(stochastic_seeds[1], (P_SIZE,), jnp.float32, jnp.log(0.05 / SNAPSHOT_TOTAL), jnp.log(0.5 / SNAPSHOT_TOTAL)))
    fast_rate = jnp.exp(jax.random.uniform(stochastic_seeds[2], (P_SIZE,), jnp.float32, jnp.log(0.3), jnp.log(1.0)))
    base_rate = jnp.where(gradual_damping, slow_rate, fast_rate)
    jitter = jnp.exp(jax.random.uniform(stochastic_seeds[3], (SNAPSHOT_TOTAL, P_SIZE), jnp.float32, -0.5, 0.5))
    entry_lines = jnp.exp(-base_rate[None, :] * jitter)
    spike_location = jax.random.randint(stochastic_seeds[4], (3,), 0, SNAPSHOT_TOTAL)
    snapshot_numbers = jnp.arange(SNAPSHOT_TOTAL)[:, None]
    spike_sequence = jnp.any(snapshot_numbers == spike_location[None, :], axis=1)
    multiplier_amount = jax.random.uniform(stochastic_seeds[5], (P_SIZE,), jnp.float32, 0.6, 0.85)
    entry_lines = jnp.where(spike_sequence[:, None] & gradual_damping[None, :], entry_lines * multiplier_amount[None, :], entry_lines)
    return jnp.clip(entry_lines, 0.01, 0.999).astype(jnp.float32)


def block_levels(own_key, shape, cuts, smallest, top_value):
    def one(axis_at, blocks):
        heights = jax.random.uniform(jax.random.fold_in(jax.random.fold_in(own_key, 6), axis_at), (blocks,), jnp.float32, smallest / len(cuts), top_value / len(cuts))
        return jnp.repeat(jnp.exp(heights), shape[axis_at] // blocks).reshape((-1,) + (1,) * (len(shape) - axis_at - 1))

    factor_of = one(*cuts[0])
    for cut in cuts[1:]:
        factor_of = factor_of * one(*cut)
    return factor_of


def bell_draw(stream_key, extent, spread, bound, cuts=(), dtype=jnp.bfloat16):
    result = jax.random.normal(stream_key, extent, jnp.float32) * spread
    if len(cuts) > 0:
        result = block_levels(stream_key, extent, cuts, -0.22, 0.18) * result
    return jnp.clip(result, min=-bound, max=bound).astype(dtype)


def setup_inputs(seed: int = 0, part: int = 0) -> dict:
    arg_keys = jax.random.split(jax.random.key(seed), 7)
    own_keys = jax.random.split(jax.random.fold_in(arg_keys[6], part), 7)
    states = bell_draw(own_keys[0], (SNAPSHOT_TOTAL, H, COLS, P_SIZE), 1.0, 6.0, ((0, 8), (1, 2)))
    inputs = bell_draw(own_keys[1], (SNAPSHOT_TOTAL, H, COLS, U), 1.0, 6.0, ((0, 8), (1, 2)))
    grad_y = bell_draw(own_keys[2], (SNAPSHOT_TOTAL, H, COLS, U), 0.1, 0.59765625, ((0, 8), (1, 2)))
    decay = draw_decay(jax.random.fold_in(jax.random.fold_in(arg_keys[6], part), 71), part)
    in_kernel = bell_draw(arg_keys[4], (9 * U, P_SIZE), (9 * U) ** -0.5, 0.125, ((0, 16),))
    out_kernel = bell_draw(arg_keys[5], (9 * P_SIZE, U), (9 * P_SIZE) ** -0.5, 0.09375, ((0, 16),))
    return dict(states=states, inputs=inputs, grad_y=grad_y, decay=decay, in_kernel=in_kernel, out_kernel=out_kernel)


tap_offsets = [(-1, -1), (-1, 0), (-1, 1), (0, -1), (0, 0), (0, 1), (1, -1), (1, 0), (1, 1)]


def shifted(field, row_step, col_step):
    padded = jnp.pad(field, ((0, 0), (1, 1), (1, 1), (0, 0)))
    height, n_cols = field.shape[1], field.shape[2]
    return padded[:, 1 + row_step:1 + row_step + height, 1 + col_step:1 + col_step + n_cols, :]


def contract_last(left_mat, right_mat):
    return lax.dot_general(left_mat, right_mat, (((1,), (1,)), ((), ())), preferred_element_type=jnp.float32)


def contract_first(left_mat, right_mat):
    return lax.dot_general(left_mat, right_mat, (((0,), (0,)), ((), ())), preferred_element_type=jnp.float32)


def back_step(carried, frame_item):
    source, decay_t = frame_item
    adjoint_t = source + carried
    return decay_t[None, None, :] * adjoint_t, adjoint_t


def reference(states, inputs, grad_y, decay, in_kernel, out_kernel):
    time_len, height, n_cols, n_chans = states.shape
    n_units = inputs.shape[3]
    num_cells = time_len * height * n_cols
    in_taps = in_kernel.reshape(9, n_units, n_chans)
    out_taps = out_kernel.reshape(9, n_chans, n_units)
    emitted = jnp.zeros((num_cells, n_chans), jnp.float32)
    for tap_id, (row_step, col_step) in enumerate(tap_offsets):
        emitted = emitted + contract_last(shifted(grad_y, -row_step, -col_step).reshape(num_cells, n_units), out_taps[tap_id])
    emitted = emitted.reshape(time_len, height, n_cols, n_chans)
    zero_state = jnp.zeros((height, n_cols, n_chans), jnp.float32)
    unused, adjoint = lax.scan(back_step, zero_state, (emitted, decay), reverse=True)
    adjoint_bf = adjoint.astype(jnp.bfloat16)
    flat_adjoint = adjoint_bf.reshape(num_cells, n_chans)
    flat_grad = grad_y.reshape(num_cells, n_units)
    grad_inputs = jnp.zeros((num_cells, n_units), jnp.float32)
    in_grads = []
    out_grads = []
    for tap_id, (row_step, col_step) in enumerate(tap_offsets):
        grad_inputs = grad_inputs + contract_last(shifted(adjoint_bf, -row_step, -col_step).reshape(num_cells, n_chans), in_taps[tap_id])
        in_grads.append(contract_first(shifted(inputs, row_step, col_step).reshape(num_cells, n_units), flat_adjoint))
        out_grads.append(contract_first(shifted(states, row_step, col_step).reshape(num_cells, n_chans), flat_grad))
    previous = jnp.concatenate([jnp.zeros_like(states[:1]), states[:-1]], 0)
    grad_decay = jnp.sum(adjoint * previous.astype(jnp.float32), axis=(1, 2))
    grad_inputs = grad_inputs.reshape(time_len, height, n_cols, n_units).astype(jnp.bfloat16)
    return grad_inputs, jnp.concatenate(in_grads, 0), jnp.concatenate(out_grads, 0), grad_decay
```

```python
import functools

import jax
import jax.numpy as jnp
from jax import lax
from jax.experimental import pallas as pl
from jax.experimental.pallas import tpu as pltpu
from jax.sharding import PartitionSpec as P

tap_offsets = [(-1, -1), (-1, 0), (-1, 1), (0, -1), (0, 0), (0, 1), (1, -1), (1, 0), (1, 1)]


def with_halo(block, sides, width):
    for axis, dim in sides:
        count = lax.axis_size(axis)
        forward = [(i, i + 1) for i in range(count - 1)]
        backward = [(target, source) for source, target in forward]
        low = lax.ppermute(
            lax.slice_in_dim(block, block.shape[dim] - width, None, axis=dim), axis, forward
        )
        high = lax.ppermute(lax.slice_in_dim(block, 0, width, axis=dim), axis, backward)
        block = jnp.concatenate([low, block, high], axis=dim)
    return block


def prefix(value, axis, join, neutral):
    count, mine = (lax.axis_size(axis), lax.axis_index(axis))
    pieces = jax.tree.map(lambda part: lax.all_gather(part, axis), value)
    pieces = jax.tree.map(lambda part: part[::-1], pieces)
    mine = count - 1 - mine
    so_far = jax.tree.map(
        lambda part, zero: jnp.full_like(part, 0) + jnp.asarray(zero, part.dtype), value, neutral
    )

    def turn(position, so_far):
        longer = join(so_far, jax.tree.map(lambda part: part[position], pieces))
        return jax.tree.map(lambda new, old: jnp.where(position < mine, new, old), longer, so_far)

    return lax.fori_loop(0, count - 1, turn, so_far)


def from_behind(shard, axis, by):
    size = lax.axis_size(axis)
    pairs = [(i, i + by) for i in range(size) if 0 <= i + by < size]
    return lax.ppermute(shard, axis, pairs)


def tap_field(extended, row_step, col_step):
    band = extended.shape[-3] - 2
    n_cols = extended.shape[-2]
    pad_spec = [(0, 0)] * (extended.ndim - 2) + [(1, 1), (0, 0)]
    padded = jnp.pad(extended, pad_spec)
    return padded[..., 1 + row_step : 1 + row_step + band, 1 + col_step : 1 + col_step + n_cols, :]


def contract_last(left_mat, right_mat):
    return lax.dot_general(
        left_mat, right_mat, (((1,), (1,)), ((), ())), preferred_element_type=jnp.float32
    )


def contract_first(left_mat, right_mat):
    return lax.dot_general(
        left_mat, right_mat, (((0,), (0,)), ((), ())), preferred_element_type=jnp.float32
    )


def back_step(carried, frame_item):
    source, decay_t = frame_item
    adjoint_t = source + carried
    return (decay_t[None, None, :] * adjoint_t, adjoint_t)


def chain_combine(earlier, later):
    return (later[0] * earlier[0], later[0][None, None, :] * earlier[1] + later[1])


def body(states, inputs, grad_y, decay, in_kernel, out_kernel):
    frames, band, n_cols, n_chans = states.shape
    n_units = inputs.shape[3]
    num_cells = frames * band * n_cols
    in_full, out_full = (
        lax.all_gather(in_kernel, ("tm", "rows"), axis=0, tiled=True),
        lax.all_gather(out_kernel, ("tm", "rows"), axis=0, tiled=True),
    )
    in_taps = in_full.reshape(9, n_units, n_chans)
    out_taps = out_full.reshape(9, n_chans, n_units)
    both_ext = with_halo(jnp.stack([grad_y, inputs]), (("rows", 2),), 1)
    grad_ext = both_ext[0]
    input_ext = both_ext[1]
    state_ext = with_halo(states, (("rows", 1),), 1)
    flat_grad = grad_y.reshape(num_cells, n_units)
    emitted = jnp.zeros((num_cells, n_chans), jnp.float32)
    out_grads = []
    for tap_id, (row_step, col_step) in enumerate(tap_offsets):
        emitted = emitted + contract_last(
            tap_field(grad_ext, -row_step, -col_step).reshape(num_cells, n_units), out_taps[tap_id]
        )
        out_grads.append(
            contract_first(
                tap_field(state_ext, row_step, col_step).reshape(num_cells, n_chans), flat_grad
            )
        )
    grad_out_local = jnp.concatenate(out_grads, 0)
    emitted = emitted.reshape(frames, band, n_cols, n_chans)
    zero_state = jnp.zeros((band, n_cols, n_chans), jnp.float32)
    summary, local_adjoint = lax.scan(back_step, zero_state, (emitted, decay), reverse=True)
    block_decay = jnp.prod(decay, axis=0)
    chained = prefix(
        (block_decay, summary),
        "tm",
        chain_combine,
        (jnp.ones_like(block_decay), jnp.zeros_like(summary)),
    )
    incoming = chained[1]
    unused, adjoint = lax.scan(back_step, incoming, (emitted, decay), reverse=True)
    adjoint_bf = adjoint.astype(jnp.bfloat16)
    adjoint_ext = with_halo(adjoint_bf, (("rows", 1),), 1)
    flat_adjoint = adjoint_bf.reshape(num_cells, n_chans)
    grad_inputs = jnp.zeros((num_cells, n_units), jnp.float32)
    in_grads = []
    for tap_id, (row_step, col_step) in enumerate(tap_offsets):
        grad_inputs = grad_inputs + contract_last(
            tap_field(adjoint_ext, -row_step, -col_step).reshape(num_cells, n_chans),
            in_taps[tap_id],
        )
        in_grads.append(
            contract_first(
                tap_field(input_ext, row_step, col_step).reshape(num_cells, n_units), flat_adjoint
            )
        )
    grad_in_local = jnp.concatenate(in_grads, 0)
    before_block = from_behind(states[-1:], "tm", 1)
    previous = jnp.concatenate([before_block, states[:-1]], 0)
    decay_part = jnp.sum(adjoint * previous.astype(jnp.float32), axis=(1, 2))
    grad_decay = lax.psum(decay_part, "rows")
    grad_in_kernel, grad_out_kernel = (
        lax.psum_scatter(grad_in_local, ("tm", "rows"), scatter_dimension=0, tiled=True),
        lax.psum_scatter(grad_out_local, ("tm", "rows"), scatter_dimension=0, tiled=True),
    )
    grad_inputs = grad_inputs.reshape(frames, band, n_cols, n_units).astype(jnp.bfloat16)
    return (grad_inputs, grad_in_kernel, grad_out_kernel, grad_decay)


def ring_kernel(
    n, st_ref, in_ref, gy_ref, dec_ref, wi_ref, wo_ref,
    gi_ref, gik_ref, gok_ref, gd_ref,
    wout, win, stt, int_, eg, ea, em, og, ig,
    hg_r, ha_s, ha_r, dall, last_r, pf_s, pf_r,
    ocs, ocr, oxs, oxr, ozs, ozr, ics, icr, ixs, ixr, izs, izr,
    gd_s, gd_r, ss, rs,
):
    f32, bf16 = jnp.float32, jnp.bfloat16
    frames, chans = dec_ref.shape
    n_cells, units = in_ref.shape
    cells = n_cells // frames
    n_cols = cells // 2
    nz = n // 2
    tm, c = lax.axis_index("tm"), lax.axis_index("rows")
    z, x = tm // 2, lax.rem(tm, 2)
    counter = [0]

    def fresh(count):
        first = counter[0]
        counter[0] += count
        return first

    def remote(src, dst, i, t, r):
        return pltpu.make_async_remote_copy(
            src_ref=src, dst_ref=dst, send_sem=ss.at[i], recv_sem=rs.at[i],
            device_id={"tm": t, "rows": r}, device_id_type=pl.DeviceIdType.MESH,
        )

    def wrap(value, size):
        return lax.rem(value + size, size)

    sends = []

    def start(*what):
        copy = remote(*what)
        copy.start()
        sends.append(copy)
        return copy

    barrier = pltpu.get_barrier_semaphore()
    me = tm * 2 + c

    def greet(step, carry):
        other = lax.rem(me + step, 2 * n)
        pl.semaphore_signal(
            barrier, inc=1, device_id={"tm": other // 2, "rows": lax.rem(other, 2)},
            device_id_type=pl.DeviceIdType.MESH,
        )
        return carry

    lax.fori_loop(1, 2 * n, greet, 0)
    pl.semaphore_wait(barrier, 2 * n - 1)

    class Gather:
        def __init__(self, own, full):
            self.own, self.full, self.rows = own, full, own.shape[0]
            self.base = fresh(4 * nz)

        def slot(self, zz, xx, cc):
            return self.full.at[pl.ds(((zz * 2 + xx) * 2 + cc) * self.rows, self.rows)]

        def begin(self):
            mine = self.slot(z, x, c)
            self.z_copies = [
                start(self.own, mine, self.base + o, wrap(z + o, nz) * 2 + x, c)
                for o in range(1, nz)
            ]
            self.x_copies = [start(self.own, mine, self.base + nz, z * 2 + 1 - x, c)]
            self.c_copies = [start(self.own, mine, self.base + 2 * nz, tm, 1 - c)]
            mine[...] = self.own[...]

        def after_z(self):
            for o in range(1, nz):
                self.z_copies[o - 1].wait_recv()
                block = self.slot(wrap(z - o, nz), x, c)
                self.x_copies.append(start(block, block, self.base + nz + o, z * 2 + 1 - x, c))
                self.c_copies.append(start(block, block, self.base + 2 * nz + o, tm, 1 - c))

        def after_x(self):
            for o in range(nz):
                self.x_copies[o].wait_recv()
                block = self.slot(wrap(z - o, nz), 1 - x, c)
                self.c_copies.append(start(block, block, self.base + 3 * nz + o, tm, 1 - c))

        def finish(self):
            for copy in self.c_copies:
                copy.wait_recv()

    class Scatter:
        def __init__(self, acc, out, cs, cr, xs, xr, zs, zr):
            self.acc, self.out, self.rows = acc, out, out.shape[0]
            self.cs, self.cr, self.xs, self.xr, self.zs, self.zr = cs, cr, xs, xr, zs, zr
            self.base = fresh(2 + nz)

        def part(self, t, cc):
            return self.acc[pl.ds((t * 2 + cc) * self.rows, self.rows), :]

        def core(self):
            def pack(t, carry):
                self.cs[t] = self.part(t, 1 - c).astype(bf16)
                return carry

            lax.fori_loop(0, n, pack, 0)
            self.c_copy = start(self.cs, self.cr, self.base, tm, 1 - c)

        def across(self):
            self.c_copy.wait_recv()

            def pack(zz, carry):
                t = zz * 2 + 1 - x
                self.xs[zz] = (self.part(t, c) + self.cr[t].astype(f32)).astype(bf16)
                return carry

            lax.fori_loop(0, nz, pack, 0)
            self.x_copy = start(self.xs, self.xr, self.base + 1, z * 2 + 1 - x, c)

        def total(self, zz):
            t = zz * 2 + x
            return self.part(t, c) + self.cr[t].astype(f32) + self.xr[zz].astype(f32)

        def along(self):
            self.x_copy.wait_recv()
            self.z_copies = []
            for o in range(1, nz):
                zz = wrap(z + o, nz)
                self.zs[o - 1] = self.total(zz).astype(bf16)
                self.z_copies.append(
                    start(self.zs.at[o - 1], self.zr.at[o - 1], self.base + 1 + o, zz * 2 + x, c)
                )

        def finish(self):
            self.out[...] = self.total(z)
            for o in range(1, nz):
                self.z_copies[o - 1].wait_recv()
                self.out[...] += self.zr[o - 1].astype(f32)

    gather_out = Gather(wo_ref, wout)
    gather_in = Gather(wi_ref, win)
    halo_sem = fresh(frames)
    halo = []
    for t in range(frames):
        row = gy_ref.at[pl.ds(t * cells + (1 - c) * n_cols, n_cols)]
        halo.append(start(row, hg_r.at[t], halo_sem + t, tm, 1 - c))
    gather_out.begin()
    dec_sem = fresh(n)
    dec_copies = [
        start(dec_ref, dall.at[tm], dec_sem + o, wrap(tm + o, n), c) for o in range(1, n)
    ]
    dall[tm] = dec_ref[...]
    last_copy = start(
        st_ref.at[pl.ds((frames - 1) * cells, cells)], last_r, fresh(1), wrap(tm + 1, n), c
    )

    def spread(ext, received, width):
        def one(t, carry):
            ext[1, t, 3 * (1 - c)] = received[t]
            ext[1, t, 3 * c] = jnp.zeros((n_cols, width), bf16)
            field = ext[1, t].astype(f32).reshape(4 * n_cols, width)
            col = lax.rem(
                lax.broadcasted_iota(jnp.int32, (4 * n_cols, width), 0), n_cols
            )
            up = jnp.where(col == 0, 0.0, pltpu.roll(field, 1, 0))
            down = jnp.where(col == n_cols - 1, 0.0, pltpu.roll(field, 4 * n_cols - 1, 0))
            ext[2, t] = up.astype(bf16).reshape(4, n_cols, width)
            ext[0, t] = down.astype(bf16).reshape(4, n_cols, width)
            return carry

        lax.fori_loop(0, frames, one, 0)

    def tap(ext, k, width):
        return ext[lax.rem(k, 3), :, pl.ds(2 - k // 3, 2)].reshape(n_cells, width)

    def last_with_last(a, b):
        return lax.dot_general(a, b, (((1,), (1,)), ((), ())), preferred_element_type=f32)

    stt[...] = st_ref[...].T
    for copy in halo:
        copy.wait_recv()
    for t in range(frames):
        eg[1, t, 1:3] = gy_ref[pl.ds(t * cells, cells), :].reshape(2, n_cols, units)
    spread(eg, hg_r, units)
    gather_out.after_z()

    def out_tap(k, carry):
        og[pl.ds(pl.multiple_of(k * chans, chans), chans), :] = jnp.dot(
            stt[...], tap(eg, k, units), preferred_element_type=f32
        )
        return carry

    lax.fori_loop(0, 9, out_tap, 0)
    scatter_out = Scatter(og, gok_ref, ocs, ocr, oxs, oxr, ozs, ozr)
    scatter_in = Scatter(ig, gik_ref, ics, icr, ixs, ixr, izs, izr)
    scatter_out.core()
    gather_out.after_x()
    gather_in.begin()
    int_[...] = in_ref[...].T
    em[...] = jnp.zeros_like(em)
    gather_out.finish()

    def emit_tap(k, carry):
        em[...] += last_with_last(
            tap(eg, k, units), wout[pl.ds(pl.multiple_of(k * chans, chans), chans), :]
        )
        return carry

    lax.fori_loop(0, 9, emit_tap, 0)

    carried = jnp.zeros((cells, chans), f32)
    for t in range(frames - 1, -1, -1):
        here = em[pl.ds(t * cells, cells), :] + carried
        em[pl.ds(t * cells, cells), :] = here
        carried = dec_ref[pl.ds(t, 1), :] * here

    for copy in dec_copies:
        copy.wait_recv()

    def block_decay(steps):
        block = dall[wrap(tm + steps, n)]
        value = block[0:1]
        for t in range(1, frames):
            value = value * block[t : t + 1]
        return value

    pf_s[0] = carried
    reach, slot, total, first = 1, 0, None, True
    extra = [scatter_out.across, gather_in.after_z]
    while True:
        offsets = [1, 2, 3] if first else [reach, 2 * reach]
        sems = fresh(len(offsets))
        copies = [
            start(pf_s.at[slot], pf_r.at[len_], sems + j, wrap(tm - d, n), c)
            for j, (d, len_) in enumerate(
                (d, (0 if first else 3) + j) for j, d in enumerate(offsets)
            )
        ]
        if extra:
            extra.pop(0)()
        weight, at = None, 1
        for j, d in enumerate(offsets):
            copies[j].wait_recv()
            while at < d + (0 if first else 1):
                factor = block_decay(at)
                weight = factor if weight is None else weight * factor
                at += 1
            item = pf_r[(0 if first else 3) + j]
            if weight is not None:
                item = weight * item
            item = jnp.where(tm + d < n, item, 0.0)
            total = item if total is None else total + item
        reach = 3 if first else 3 * reach
        if reach >= n - 1:
            break
        first = False
        slot += 1
        pf_s[slot] = total
    pf_s[slot + 1] = total
    while extra:
        extra.pop(0)()

    factor = None
    for t in range(frames - 1, -1, -1):
        add = pf_s[slot + 1]
        if factor is not None:
            add = factor * add
        here = em[pl.ds(t * cells, cells), :] + add
        em[pl.ds(t * cells, cells), :] = here
        rounded = here.astype(bf16).reshape(2, n_cols, chans)
        ea[1, t, 1:3] = rounded
        row = dec_ref[pl.ds(t, 1), :]
        factor = row if factor is None else factor * row

    def edge(t, carry):
        ha_s[t] = ea[1, t, 2 - c]
        return carry

    lax.fori_loop(0, frames, edge, 0)
    adj_copy = start(ha_s, ha_r, fresh(1), tm, 1 - c)

    last_copy.wait_recv()
    rows = []
    for t in range(frames):
        if t == 0:
            before = jnp.where(tm > 0, last_r[...].astype(f32), 0.0)
        else:
            before = st_ref[pl.ds((t - 1) * cells, cells), :].astype(f32)
        gd_s[pl.ds(t, 1), :] = jnp.sum(
            em[pl.ds(t * cells, cells), :] * before, axis=0, keepdims=True
        )
    gd_copy = start(gd_s, gd_r, fresh(1), tm, 1 - c)

    adj_copy.wait_recv()
    spread(ea, ha_r, chans)

    def in_tap(k, carry):
        ig[pl.ds(pl.multiple_of(k * units, units), units), :] = jnp.dot(
            int_[...], tap(ea, k, chans), preferred_element_type=f32
        )
        return carry

    lax.fori_loop(0, 9, in_tap, 0)
    scatter_in.core()
    scatter_out.along()
    scatter_in.across()
    gather_in.after_x()
    gather_in.finish()
    em[:, :units] = jnp.zeros((n_cells, units), f32)

    def back_tap(k, carry):
        em[:, :units] += last_with_last(
            tap(ea, k, chans), win[pl.ds(pl.multiple_of(k * units, units), units), :]
        )
        return carry

    lax.fori_loop(0, 9, back_tap, 0)
    scatter_in.along()
    gi_ref[...] = em[:, :units].astype(bf16)
    gd_copy.wait_recv()
    gd_ref[...] = gd_s[...] + gd_r[...]
    scatter_out.finish()
    scatter_in.finish()
    for copy in sends:
        copy.wait_send()


def fused_body(states, inputs, grad_y, decay, in_kernel, out_kernel):
    frames, band, n_cols, chans = states.shape
    units = inputs.shape[3]
    n = lax.axis_size("tm")
    nz = n // 2
    cells = band * n_cols
    n_cells = frames * cells
    ri, ro = in_kernel.shape[0], out_kernel.shape[0]
    f32, bf16 = jnp.float32, jnp.bfloat16
    V = pltpu.VMEM
    n_sems = 128
    outs = pl.pallas_call(
        functools.partial(ring_kernel, n),
        out_shape=(
            jax.ShapeDtypeStruct((n_cells, units), bf16),
            jax.ShapeDtypeStruct((ri, chans), f32),
            jax.ShapeDtypeStruct((ro, units), f32),
            jax.ShapeDtypeStruct((frames, chans), f32),
        ),
        in_specs=[pl.BlockSpec(memory_space=pltpu.VMEM)] * 6,
        out_specs=tuple([pl.BlockSpec(memory_space=pltpu.VMEM)] * 4),
        scratch_shapes=[
            V((9 * chans, units), bf16),
            V((9 * units, chans), bf16),
            V((chans, n_cells), bf16),
            V((units, n_cells), bf16),
            V((3, frames, 4, n_cols, units), bf16),
            V((3, frames, 4, n_cols, chans), bf16),
            V((n_cells, chans), f32),
            V((9 * chans, units), f32),
            V((9 * units, chans), f32),
            V((frames, n_cols, units), bf16),
            V((frames, n_cols, chans), bf16),
            V((frames, n_cols, chans), bf16),
            V((n, frames, chans), f32),
            V((cells, chans), bf16),
            V((3, cells, chans), f32),
            V((5, cells, chans), f32),
        ]
        + [
            V(shape, bf16)
            for r, w in ((ro, units), (ri, chans))
            for shape in (
                (n, r, w), (n, r, w), (nz, r, w), (nz, r, w), (nz - 1, r, w), (nz - 1, r, w),
            )
        ]
        + [
            V((frames, chans), f32),
            V((frames, chans), f32),
            pltpu.SemaphoreType.DMA((n_sems,)),
            pltpu.SemaphoreType.DMA((n_sems,)),
        ],
        compiler_params=pltpu.CompilerParams(
            collective_id=0, has_side_effects=True, vmem_limit_bytes=52 << 20
        ),
    )(
        states.reshape(n_cells, chans),
        inputs.reshape(n_cells, units),
        grad_y.reshape(n_cells, units),
        decay,
        in_kernel,
        out_kernel,
    )
    return (outs[0].reshape(frames, band, n_cols, units),) + tuple(outs[1:])


def one_device(*arrays):
    states, in_kernel, out_kernel = arrays[0], arrays[4], arrays[5]
    n = lax.axis_size("tm")
    fits = (
        n % 2 == 0 and 4 <= n <= 10 and lax.axis_size("rows") == 2
        and states.shape[1] == 2 and states.shape[0] == 8
        and in_kernel.shape[0] % 16 == 0 and out_kernel.shape[0] % 16 == 0
    )
    return fused_body(*arrays) if fits else body(*arrays)


def solution(mesh):
    return jax.shard_map(
        one_device,
        mesh=mesh,
        in_specs=(
            P(("groups", "tm"), "rows", None, None),
            P(("groups", "tm"), "rows", None, None),
            P(("groups", "tm"), "rows", None, None),
            P(("groups", "tm"), None),
            P(("tm", "rows"), None),
            P(("tm", "rows"), None),
        ),
        out_specs=(
            P(("groups", "tm"), "rows", None, None),
            P(("groups", "tm", "rows"), None),
            P(("groups", "tm", "rows"), None),
            P(("groups", "tm"), None),
        ),
        check_vma=False,
    )
```

```python
import functools

import jax
import jax.numpy as jnp
from jax import lax
from jax.experimental import pallas as pl
from jax.experimental.pallas import tpu as pltpu
from jax.sharding import PartitionSpec as P

tap_offsets = [(-1, -1), (-1, 0), (-1, 1), (0, -1), (0, 0), (0, 1), (1, -1), (1, 0), (1, 1)]


def with_halo(block, sides, width):
    for axis, dim in sides:
        count = lax.axis_size(axis)
        forward = [(i, i + 1) for i in range(count - 1)]
        backward = [(target, source) for source, target in forward]
        low = lax.ppermute(
            lax.slice_in_dim(block, block.shape[dim] - width, None, axis=dim), axis, forward
        )
        high = lax.ppermute(lax.slice_in_dim(block, 0, width, axis=dim), axis, backward)
        block = jnp.concatenate([low, block, high], axis=dim)
    return block


def prefix(value, axis, join, neutral):
    count, mine = (lax.axis_size(axis), lax.axis_index(axis))
    pieces = jax.tree.map(lambda part: lax.all_gather(part, axis), value)
    pieces = jax.tree.map(lambda part: part[::-1], pieces)
    mine = count - 1 - mine
    so_far = jax.tree.map(
        lambda part, zero: jnp.full_like(part, 0) + jnp.asarray(zero, part.dtype), value, neutral
    )

    def turn(position, so_far):
        longer = join(so_far, jax.tree.map(lambda part: part[position], pieces))
        return jax.tree.map(lambda new, old: jnp.where(position < mine, new, old), longer, so_far)

    return lax.fori_loop(0, count - 1, turn, so_far)


def from_behind(shard, axis, by):
    size = lax.axis_size(axis)
    pairs = [(i, i + by) for i in range(size) if 0 <= i + by < size]
    return lax.ppermute(shard, axis, pairs)


def tap_field(extended, row_step, col_step):
    band = extended.shape[-3] - 2
    n_cols = extended.shape[-2]
    pad_spec = [(0, 0)] * (extended.ndim - 2) + [(1, 1), (0, 0)]
    padded = jnp.pad(extended, pad_spec)
    return padded[..., 1 + row_step : 1 + row_step + band, 1 + col_step : 1 + col_step + n_cols, :]


def contract_last(left_mat, right_mat):
    return lax.dot_general(
        left_mat, right_mat, (((1,), (1,)), ((), ())), preferred_element_type=jnp.float32
    )


def contract_first(left_mat, right_mat):
    return lax.dot_general(
        left_mat, right_mat, (((0,), (0,)), ((), ())), preferred_element_type=jnp.float32
    )


def back_step(carried, frame_item):
    source, decay_t = frame_item
    adjoint_t = source + carried
    return (decay_t[None, None, :] * adjoint_t, adjoint_t)


def chain_combine(earlier, later):
    return (later[0] * earlier[0], later[0][None, None, :] * earlier[1] + later[1])


def body(states, inputs, grad_y, decay, in_kernel, out_kernel):
    frames, band, n_cols, n_chans = states.shape
    n_units = inputs.shape[3]
    num_cells = frames * band * n_cols
    in_full, out_full = (
        lax.all_gather(in_kernel, ("tm", "rows"), axis=0, tiled=True),
        lax.all_gather(out_kernel, ("tm", "rows"), axis=0, tiled=True),
    )
    in_taps = in_full.reshape(9, n_units, n_chans)
    out_taps = out_full.reshape(9, n_chans, n_units)
    both_ext = with_halo(jnp.stack([grad_y, inputs]), (("rows", 2),), 1)
    grad_ext = both_ext[0]
    input_ext = both_ext[1]
    state_ext = with_halo(states, (("rows", 1),), 1)
    flat_grad = grad_y.reshape(num_cells, n_units)
    emitted = jnp.zeros((num_cells, n_chans), jnp.float32)
    out_grads = []
    for tap_id, (row_step, col_step) in enumerate(tap_offsets):
        emitted = emitted + contract_last(
            tap_field(grad_ext, -row_step, -col_step).reshape(num_cells, n_units), out_taps[tap_id]
        )
        out_grads.append(
            contract_first(
                tap_field(state_ext, row_step, col_step).reshape(num_cells, n_chans), flat_grad
            )
        )
    grad_out_local = jnp.concatenate(out_grads, 0)
    emitted = emitted.reshape(frames, band, n_cols, n_chans)
    zero_state = jnp.zeros((band, n_cols, n_chans), jnp.float32)
    summary, local_adjoint = lax.scan(back_step, zero_state, (emitted, decay), reverse=True)
    block_decay = jnp.prod(decay, axis=0)
    chained = prefix(
        (block_decay, summary),
        "tm",
        chain_combine,
        (jnp.ones_like(block_decay), jnp.zeros_like(summary)),
    )
    incoming = chained[1]
    unused, adjoint = lax.scan(back_step, incoming, (emitted, decay), reverse=True)
    adjoint_bf = adjoint.astype(jnp.bfloat16)
    adjoint_ext = with_halo(adjoint_bf, (("rows", 1),), 1)
    flat_adjoint = adjoint_bf.reshape(num_cells, n_chans)
    grad_inputs = jnp.zeros((num_cells, n_units), jnp.float32)
    in_grads = []
    for tap_id, (row_step, col_step) in enumerate(tap_offsets):
        grad_inputs = grad_inputs + contract_last(
            tap_field(adjoint_ext, -row_step, -col_step).reshape(num_cells, n_chans),
            in_taps[tap_id],
        )
        in_grads.append(
            contract_first(
                tap_field(input_ext, row_step, col_step).reshape(num_cells, n_units), flat_adjoint
            )
        )
    grad_in_local = jnp.concatenate(in_grads, 0)
    before_block = from_behind(states[-1:], "tm", 1)
    previous = jnp.concatenate([before_block, states[:-1]], 0)
    decay_part = jnp.sum(adjoint * previous.astype(jnp.float32), axis=(1, 2))
    grad_decay = lax.psum(decay_part, "rows")
    grad_in_kernel, grad_out_kernel = (
        lax.psum_scatter(grad_in_local, ("tm", "rows"), scatter_dimension=0, tiled=True),
        lax.psum_scatter(grad_out_local, ("tm", "rows"), scatter_dimension=0, tiled=True),
    )
    grad_inputs = grad_inputs.reshape(frames, band, n_cols, n_units).astype(jnp.bfloat16)
    return (grad_inputs, grad_in_kernel, grad_out_kernel, grad_decay)


def ring_kernel(
    n, st_hbm, in_hbm, gy_hbm, dec_hbm, wi_ref, wo_ref,
    gi_ref, gik_ref, gok_ref, gd_ref,
    wout, win, stt, int_, eg, ea, em, og, ig,
    hg_r, ha_s, ha_r, dall, last_r, pf_s, pf_r,
    ocs, ocr, oxs, oxr, ozs, ozr, ics, icr, ixs, ixr, izs, izr,
    gd_s, gd_r, st_ref, in_ref, gy_ref, dec_ref, ss, rs, ls,
):
    f32, bf16 = jnp.float32, jnp.bfloat16
    frames, chans = dec_ref.shape
    n_cells, units = in_ref.shape
    cells = n_cells // frames
    n_cols = cells // 2
    nz = n // 2
    tm, c = lax.axis_index("tm"), lax.axis_index("rows")
    g = lax.axis_index("groups")
    z, x = tm // 2, lax.rem(tm, 2)
    counter = [0]

    def fresh(count):
        first = counter[0]
        counter[0] += count
        return first

    def remote(src, dst, i, t, r, away=None):
        return pltpu.make_async_remote_copy(
            src_ref=src, dst_ref=dst, send_sem=ss.at[i], recv_sem=rs.at[i],
            device_id={"groups": g if away is None else away, "tm": t, "rows": r},
            device_id_type=pl.DeviceIdType.MESH,
        )

    local = [
        pltpu.make_async_copy(src, dst, ls.at[i])
        for i, (src, dst) in enumerate(
            ((gy_hbm, gy_ref), (st_hbm, st_ref), (in_hbm, in_ref), (dec_hbm, dec_ref))
        )
    ]
    for copy in local:
        copy.start()

    def wrap(value, size):
        return lax.rem(value + size, size)

    sends = []

    def start(*what):
        copy = remote(*what)
        copy.start()
        sends.append(copy)
        return copy

    barrier = pltpu.get_barrier_semaphore()
    me = tm * 2 + c

    def greet(step, carry):
        other = lax.rem(me + step, 2 * n)
        pl.semaphore_signal(
            barrier, inc=1, device_id={"tm": other // 2, "rows": lax.rem(other, 2)},
            device_id_type=pl.DeviceIdType.MESH,
        )
        return carry

    lax.fori_loop(1, 2 * n, greet, 0)
    pl.semaphore_signal(
        barrier, inc=1, device_id={"groups": 1 - g, "tm": tm, "rows": c},
        device_id_type=pl.DeviceIdType.MESH,
    )
    pl.semaphore_wait(barrier, 2 * n)

    class Gather:
        def __init__(self, own, full, own_sem, by_rows):
            self.own, self.full, self.rows = own, full, own.shape[0]
            self.base, self.by_rows = fresh(6 * nz), by_rows
            self.place = pltpu.make_async_copy(own, self.slot(z, x, c), ls.at[own_sem])

        def slot(self, zz, xx, cc):
            return self.full.at[pl.ds(((zz * 2 + xx) * 2 + cc) * self.rows, self.rows)]

        def part(self, ref):
            if self.by_rows:
                third = self.rows // 3
                return ref.at[pl.ds(g * third, 2 * third)]
            half = self.full.shape[1] // 2
            return ref.at[:, pl.ds(pl.multiple_of(g * half, half), half)]

        def rest(self, ref):
            if self.by_rows:
                third = self.rows // 3
                return ref.at[pl.ds(2 * g * third, third)]
            return self.part(ref)

        def y_send(self, block, i):
            rest = self.rest(block)
            self.y_copies.append(start(rest, rest, self.base + 2 * nz + i, tm, c, 1 - g))

        def x_send(self, src, block, i):
            self.x_copies.append(
                start(self.part(src), self.part(block), self.base + nz + i, z * 2 + 1 - x, c)
            )

        def begin(self):
            mine = self.slot(z, x, c)
            self.place.start()
            self.x_copies, self.y_copies, self.c_copies = [], [], []
            self.z_copies = [
                start(
                    self.part(self.own), self.part(mine), self.base + o,
                    wrap(z + o, nz) * 2 + x, c,
                )
                for o in range(1, nz)
            ]
            self.x_send(self.own, mine, 0)
            self.c_copies = [start(self.own, mine, self.base + 4 * nz, tm, 1 - c)]

        def after_z(self):
            for o in range(1, nz):
                self.z_copies[o - 1].wait_recv()
                block = self.slot(wrap(z - o, nz), x, c)
                self.y_send(block, o)
                self.x_send(block, block, o)

        def after_x(self):
            for o in range(nz):
                self.x_copies[o].wait_recv()
                self.y_send(self.slot(wrap(z - o, nz), 1 - x, c), nz + o)

        def after_y(self):
            for i in range(1, 2 * nz):
                self.y_copies[i - 1].wait_recv()
                block = self.slot(wrap(z - i % nz, nz), x if i < nz else 1 - x, c)
                self.c_copies.append(start(block, block, self.base + 4 * nz + i, tm, 1 - c))

        def finish(self):
            for copy in self.c_copies:
                copy.wait_recv()
            self.place.wait()

    class Scatter:
        def __init__(self, acc, out, cs, cr, xs, xr, zs, zr):
            self.acc, self.out, self.rows = acc, out, out.shape[0]
            self.cs, self.cr, self.xs, self.xr, self.zs, self.zr = cs, cr, xs, xr, zs, zr
            self.base = fresh(2 * nz)

        def part(self, t, cc):
            return self.acc[pl.ds((t * 2 + cc) * self.rows, self.rows), :]

        def core(self):
            def pack(t, carry):
                self.cs[t] = self.part(t, 1 - c).astype(bf16)
                return carry

            lax.fori_loop(0, n, pack, 0)
            self.c_copy = start(self.cs, self.cr, self.base, tm, 1 - c)

        def across(self):
            self.c_copy.wait_recv()
            self.x_copies = []
            for o in range(1, nz + 1):
                t = wrap(z + o, nz) * 2 + 1 - x
                self.xs[o - 1] = (self.part(t, c) + self.cr[t].astype(f32)).astype(bf16)
                self.x_copies.append(
                    start(
                        self.xs.at[o - 1], self.xr.at[o - 1], self.base + o, z * 2 + 1 - x, c
                    )
                )

        def total(self, o):
            t = wrap(z + o, nz) * 2 + x
            return self.part(t, c) + self.cr[t].astype(f32) + self.xr[o - 1].astype(f32)

        def along(self):
            self.z_copies = []
            for o in range(1, nz):
                self.x_copies[o - 1].wait_recv()
                self.zs[o - 1] = self.total(o).astype(bf16)
                self.z_copies.append(
                    start(
                        self.zs.at[o - 1], self.zr.at[o - 1], self.base + nz + o,
                        wrap(z + o, nz) * 2 + x, c,
                    )
                )
            self.x_copies[nz - 1].wait_recv()
            self.out[...] = self.total(nz)

        def finish(self):
            for o in range(1, nz):
                self.z_copies[o - 1].wait_recv()
                self.out[...] += self.zr[o - 1].astype(f32)

    gather_out = Gather(wo_ref, wout, 4, True)
    gather_in = Gather(wi_ref, win, 5, False)
    halo_sem = fresh(frames)
    halo = []
    for t in range(frames):
        row = gy_hbm.at[pl.ds(t * cells + (1 - c) * n_cols, n_cols)]
        halo.append(start(row, hg_r.at[t], halo_sem + t, tm, 1 - c))
    gather_out.begin()
    dec_sem = fresh(n)
    dec_copies = [
        start(dec_hbm, dall.at[tm], dec_sem + o, wrap(tm + o, n), c) for o in range(1, n)
    ]
    last_copy = start(
        st_hbm.at[pl.ds((frames - 1) * cells, cells)], last_r, fresh(1), wrap(tm + 1, n), c
    )

    def spread(ext, received, width):
        def one(t, carry):
            ext[1, t, 3 * (1 - c)] = received[t]
            ext[1, t, 3 * c] = jnp.zeros((n_cols, width), bf16)
            field = ext[1, t].astype(f32).reshape(4 * n_cols, width)
            col = lax.rem(
                lax.broadcasted_iota(jnp.int32, (4 * n_cols, width), 0), n_cols
            )
            up = jnp.where(col == 0, 0.0, pltpu.roll(field, 1, 0))
            down = jnp.where(col == n_cols - 1, 0.0, pltpu.roll(field, 4 * n_cols - 1, 0))
            ext[2, t] = up.astype(bf16).reshape(4, n_cols, width)
            ext[0, t] = down.astype(bf16).reshape(4, n_cols, width)
            return carry

        lax.fori_loop(0, frames, one, 0)

    def tap(ext, k, width):
        return ext[lax.rem(k, 3), :, pl.ds(2 - k // 3, 2)].reshape(n_cells, width)

    def last_with_last(a, b):
        return lax.dot_general(a, b, (((1,), (1,)), ((), ())), preferred_element_type=f32)

    for copy in local:
        copy.wait()
    dall[tm] = dec_ref[...]
    stt[...] = st_ref[...].T
    int_[...] = in_ref[...].T
    for copy in halo:
        copy.wait_recv()
    for t in range(frames):
        eg[1, t, 1:3] = gy_ref[pl.ds(t * cells, cells), :].reshape(2, n_cols, units)
    spread(eg, hg_r, units)
    gather_out.after_z()

    def out_tap(k, carry):
        og[pl.ds(pl.multiple_of(k * chans, chans), chans), :] = jnp.dot(
            stt[...], tap(eg, k, units), preferred_element_type=f32
        )
        return carry

    lax.fori_loop(0, 9, out_tap, 0)
    scatter_out = Scatter(og, gok_ref, ocs, ocr, oxs, oxr, ozs, ozr)
    scatter_in = Scatter(ig, gik_ref, ics, icr, ixs, ixr, izs, izr)
    scatter_out.core()
    gather_out.after_x()
    scatter_out.across()
    em[...] = jnp.zeros_like(em)
    gather_out.after_y()
    gather_in.begin()
    gather_out.finish()

    def emit_tap(k, carry):
        em[...] += last_with_last(
            tap(eg, k, units), wout[pl.ds(pl.multiple_of(k * chans, chans), chans), :]
        )
        return carry

    lax.fori_loop(0, 9, emit_tap, 0)

    carried = jnp.zeros((cells, chans), f32)
    for t in range(frames - 1, -1, -1):
        here = em[pl.ds(t * cells, cells), :] + carried
        em[pl.ds(t * cells, cells), :] = here
        carried = dec_ref[pl.ds(t, 1), :] * here

    for copy in dec_copies:
        copy.wait_recv()

    def block_decay(steps):
        block = dall[wrap(tm + steps, n)]
        value = block[0:1]
        for t in range(1, frames):
            value = value * block[t : t + 1]
        return value

    pf_s[0] = carried.astype(bf16)
    reach, slot, total, first = 1, 0, None, True
    extra = [gather_in.after_z]
    while True:
        offsets = [1, 2, 3] if first else [reach, 2 * reach]
        sems = fresh(len(offsets))
        copies = [
            start(pf_s.at[slot], pf_r.at[len_], sems + j, wrap(tm - d, n), c)
            for j, (d, len_) in enumerate(
                (d, (0 if first else 3) + j) for j, d in enumerate(offsets)
            )
        ]
        if extra:
            extra.pop(0)()
        weight, at = None, 1
        for j, d in enumerate(offsets):
            copies[j].wait_recv()
            while at < d + (0 if first else 1):
                factor = block_decay(at)
                weight = factor if weight is None else weight * factor
                at += 1
            item = pf_r[(0 if first else 3) + j].astype(f32)
            if weight is not None:
                item = weight * item
            item = jnp.where(tm + d < n, item, 0.0)
            total = item if total is None else total + item
        reach = 3 if first else 3 * reach
        if reach >= n - 1:
            break
        first = False
        slot += 1
        pf_s[slot] = total.astype(bf16)
    em_in = total
    while extra:
        extra.pop(0)()

    factor = None
    for t in range(frames - 1, -1, -1):
        add = em_in
        if factor is not None:
            add = factor * add
        here = em[pl.ds(t * cells, cells), :] + add
        em[pl.ds(t * cells, cells), :] = here
        rounded = here.astype(bf16).reshape(2, n_cols, chans)
        ea[1, t, 1:3] = rounded
        row = dec_ref[pl.ds(t, 1), :]
        factor = row if factor is None else factor * row

    def edge(t, carry):
        ha_s[t] = ea[1, t, 2 - c]
        return carry

    lax.fori_loop(0, frames, edge, 0)
    adj_copy = start(ha_s, ha_r, fresh(1), tm, 1 - c)

    gather_in.after_x()
    last_copy.wait_recv()
    for t in range(frames):
        if t == 0:
            before = jnp.where(tm > 0, last_r[...].astype(f32), 0.0)
        else:
            before = st_ref[pl.ds((t - 1) * cells, cells), :].astype(f32)
        gd_s[pl.ds(t, 1), :] = jnp.sum(
            em[pl.ds(t * cells, cells), :] * before, axis=0, keepdims=True
        )
    gd_copy = start(gd_s, gd_r, fresh(1), tm, 1 - c)

    scatter_out.along()
    adj_copy.wait_recv()
    spread(ea, ha_r, chans)

    def in_tap(k, carry):
        ig[pl.ds(pl.multiple_of(k * units, units), units), :] = jnp.dot(
            int_[...], tap(ea, k, chans), preferred_element_type=f32
        )
        return carry

    lax.fori_loop(0, 9, in_tap, 0)
    scatter_in.core()
    scatter_in.across()
    gather_in.after_y()
    gather_in.finish()
    em[:, :units] = jnp.zeros((n_cells, units), f32)

    def back_tap(k, carry):
        em[:, :units] += last_with_last(
            tap(ea, k, chans), win[pl.ds(pl.multiple_of(k * units, units), units), :]
        )
        return carry

    lax.fori_loop(0, 9, back_tap, 0)
    scatter_in.along()
    gi_ref[...] = em[:, :units].astype(bf16)
    gd_copy.wait_recv()
    gd_ref[...] = gd_s[...] + gd_r[...]
    scatter_out.finish()
    scatter_in.finish()
    for copy in sends:
        copy.wait_send()


def fused_body(states, inputs, grad_y, decay, in_kernel, out_kernel):
    frames, band, n_cols, chans = states.shape
    units = inputs.shape[3]
    n = lax.axis_size("tm")
    nz = n // 2
    cells = band * n_cols
    n_cells = frames * cells
    ri, ro = in_kernel.shape[0], out_kernel.shape[0]
    f32, bf16 = jnp.float32, jnp.bfloat16
    V = pltpu.VMEM
    n_sems = 128
    outs = pl.pallas_call(
        functools.partial(ring_kernel, n),
        out_shape=(
            jax.ShapeDtypeStruct((n_cells, units), bf16),
            jax.ShapeDtypeStruct((ri, chans), f32),
            jax.ShapeDtypeStruct((ro, units), f32),
            jax.ShapeDtypeStruct((frames, chans), f32),
        ),
        in_specs=[pl.BlockSpec(memory_space=pltpu.HBM)] * 6,
        out_specs=tuple([pl.BlockSpec(memory_space=pltpu.VMEM)] * 4),
        scratch_shapes=[
            V((9 * chans, units), bf16),
            V((9 * units, chans), bf16),
            V((chans, n_cells), bf16),
            V((units, n_cells), bf16),
            V((3, frames, 4, n_cols, units), bf16),
            V((3, frames, 4, n_cols, chans), bf16),
            V((n_cells, chans), f32),
            V((9 * chans, units), f32),
            V((9 * units, chans), f32),
            V((frames, n_cols, units), bf16),
            V((frames, n_cols, chans), bf16),
            V((frames, n_cols, chans), bf16),
            V((n, frames, chans), f32),
            V((cells, chans), bf16),
            V((2, cells, chans), bf16),
            V((5, cells, chans), bf16),
        ]
        + [
            V(shape, bf16)
            for r, w in ((ro, units), (ri, chans))
            for shape in (
                (n, r, w), (n, r, w), (nz, r, w), (nz, r, w), (nz - 1, r, w), (nz - 1, r, w),
            )
        ]
        + [
            V((frames, chans), f32),
            V((frames, chans), f32),
            V((n_cells, chans), bf16),
            V((n_cells, units), bf16),
            V((n_cells, units), bf16),
            V((frames, chans), f32),
            pltpu.SemaphoreType.DMA((n_sems,)),
            pltpu.SemaphoreType.DMA((n_sems,)),
            pltpu.SemaphoreType.DMA((6,)),
        ],
        compiler_params=pltpu.CompilerParams(
            collective_id=0, has_side_effects=True, vmem_limit_bytes=52 << 20
        ),
    )(
        states.reshape(n_cells, chans),
        inputs.reshape(n_cells, units),
        grad_y.reshape(n_cells, units),
        decay,
        in_kernel,
        out_kernel,
    )
    return (outs[0].reshape(frames, band, n_cols, units),) + tuple(outs[1:])


def one_device(*arrays):
    states, in_kernel, out_kernel = arrays[0], arrays[4], arrays[5]
    n = lax.axis_size("tm")
    fits = (
        n % 2 == 0 and 4 <= n <= 10 and lax.axis_size("rows") == 2
        and states.shape[1] == 2 and states.shape[0] == 8
        and lax.axis_size("groups") == 2 and states.shape[3] % 256 == 0
        and in_kernel.shape[0] % 16 == 0 and out_kernel.shape[0] % 48 == 0
    )
    return fused_body(*arrays) if fits else body(*arrays)


def solution(mesh):
    return jax.shard_map(
        one_device,
        mesh=mesh,
        in_specs=(
            P(("groups", "tm"), "rows", None, None),
            P(("groups", "tm"), "rows", None, None),
            P(("groups", "tm"), "rows", None, None),
            P(("groups", "tm"), None),
            P(("tm", "rows"), None),
            P(("tm", "rows"), None),
        ),
        out_specs=(
            P(("groups", "tm"), "rows", None, None),
            P(("groups", "tm", "rows"), None),
            P(("groups", "tm", "rows"), None),
            P(("groups", "tm"), None),
        ),
        check_vma=False,
    )
```

```python
import functools

import jax
import jax.numpy as jnp
from jax import lax
from jax.experimental import pallas as pl
from jax.experimental.pallas import tpu as pltpu
from jax.sharding import PartitionSpec as P

tap_offsets = [(-1, -1), (-1, 0), (-1, 1), (0, -1), (0, 0), (0, 1), (1, -1), (1, 0), (1, 1)]


def with_halo(block, sides, width):
    for axis, dim in sides:
        count = lax.axis_size(axis)
        forward = [(i, i + 1) for i in range(count - 1)]
        backward = [(target, source) for source, target in forward]
        low = lax.ppermute(
            lax.slice_in_dim(block, block.shape[dim] - width, None, axis=dim), axis, forward
        )
        high = lax.ppermute(lax.slice_in_dim(block, 0, width, axis=dim), axis, backward)
        block = jnp.concatenate([low, block, high], axis=dim)
    return block


def prefix(value, axis, join, neutral):
    count, mine = (lax.axis_size(axis), lax.axis_index(axis))
    pieces = jax.tree.map(lambda part: lax.all_gather(part, axis), value)
    pieces = jax.tree.map(lambda part: part[::-1], pieces)
    mine = count - 1 - mine
    so_far = jax.tree.map(
        lambda part, zero: jnp.full_like(part, 0) + jnp.asarray(zero, part.dtype), value, neutral
    )

    def turn(position, so_far):
        longer = join(so_far, jax.tree.map(lambda part: part[position], pieces))
        return jax.tree.map(lambda new, old: jnp.where(position < mine, new, old), longer, so_far)

    return lax.fori_loop(0, count - 1, turn, so_far)


def from_behind(shard, axis, by):
    size = lax.axis_size(axis)
    pairs = [(i, i + by) for i in range(size) if 0 <= i + by < size]
    return lax.ppermute(shard, axis, pairs)


def tap_field(extended, row_step, col_step):
    band = extended.shape[-3] - 2
    n_cols = extended.shape[-2]
    pad_spec = [(0, 0)] * (extended.ndim - 2) + [(1, 1), (0, 0)]
    padded = jnp.pad(extended, pad_spec)
    return padded[..., 1 + row_step : 1 + row_step + band, 1 + col_step : 1 + col_step + n_cols, :]


def contract_last(left_mat, right_mat):
    return lax.dot_general(
        left_mat, right_mat, (((1,), (1,)), ((), ())), preferred_element_type=jnp.float32
    )


def contract_first(left_mat, right_mat):
    return lax.dot_general(
        left_mat, right_mat, (((0,), (0,)), ((), ())), preferred_element_type=jnp.float32
    )


def back_step(carried, frame_item):
    source, decay_t = frame_item
    adjoint_t = source + carried
    return (decay_t[None, None, :] * adjoint_t, adjoint_t)


def chain_combine(earlier, later):
    return (later[0] * earlier[0], later[0][None, None, :] * earlier[1] + later[1])


def body(states, inputs, grad_y, decay, in_kernel, out_kernel):
    frames, band, n_cols, n_chans = states.shape
    n_units = inputs.shape[3]
    num_cells = frames * band * n_cols
    in_full, out_full = (
        lax.all_gather(in_kernel, ("tm", "rows"), axis=0, tiled=True),
        lax.all_gather(out_kernel, ("tm", "rows"), axis=0, tiled=True),
    )
    in_taps = in_full.reshape(9, n_units, n_chans)
    out_taps = out_full.reshape(9, n_chans, n_units)
    both_ext = with_halo(jnp.stack([grad_y, inputs]), (("rows", 2),), 1)
    grad_ext = both_ext[0]
    input_ext = both_ext[1]
    state_ext = with_halo(states, (("rows", 1),), 1)
    flat_grad = grad_y.reshape(num_cells, n_units)
    emitted = jnp.zeros((num_cells, n_chans), jnp.float32)
    out_grads = []
    for tap_id, (row_step, col_step) in enumerate(tap_offsets):
        emitted = emitted + contract_last(
            tap_field(grad_ext, -row_step, -col_step).reshape(num_cells, n_units), out_taps[tap_id]
        )
        out_grads.append(
            contract_first(
                tap_field(state_ext, row_step, col_step).reshape(num_cells, n_chans), flat_grad
            )
        )
    grad_out_local = jnp.concatenate(out_grads, 0)
    emitted = emitted.reshape(frames, band, n_cols, n_chans)
    zero_state = jnp.zeros((band, n_cols, n_chans), jnp.float32)
    summary, local_adjoint = lax.scan(back_step, zero_state, (emitted, decay), reverse=True)
    block_decay = jnp.prod(decay, axis=0)
    chained = prefix(
        (block_decay, summary),
        "tm",
        chain_combine,
        (jnp.ones_like(block_decay), jnp.zeros_like(summary)),
    )
    incoming = chained[1]
    unused, adjoint = lax.scan(back_step, incoming, (emitted, decay), reverse=True)
    adjoint_bf = adjoint.astype(jnp.bfloat16)
    adjoint_ext = with_halo(adjoint_bf, (("rows", 1),), 1)
    flat_adjoint = adjoint_bf.reshape(num_cells, n_chans)
    grad_inputs = jnp.zeros((num_cells, n_units), jnp.float32)
    in_grads = []
    for tap_id, (row_step, col_step) in enumerate(tap_offsets):
        grad_inputs = grad_inputs + contract_last(
            tap_field(adjoint_ext, -row_step, -col_step).reshape(num_cells, n_chans),
            in_taps[tap_id],
        )
        in_grads.append(
            contract_first(
                tap_field(input_ext, row_step, col_step).reshape(num_cells, n_units), flat_adjoint
            )
        )
    grad_in_local = jnp.concatenate(in_grads, 0)
    before_block = from_behind(states[-1:], "tm", 1)
    previous = jnp.concatenate([before_block, states[:-1]], 0)
    decay_part = jnp.sum(adjoint * previous.astype(jnp.float32), axis=(1, 2))
    grad_decay = lax.psum(decay_part, "rows")
    grad_in_kernel, grad_out_kernel = (
        lax.psum_scatter(grad_in_local, ("tm", "rows"), scatter_dimension=0, tiled=True),
        lax.psum_scatter(grad_out_local, ("tm", "rows"), scatter_dimension=0, tiled=True),
    )
    grad_inputs = grad_inputs.reshape(frames, band, n_cols, n_units).astype(jnp.bfloat16)
    return (grad_inputs, grad_in_kernel, grad_out_kernel, grad_decay)


def ring_kernel(
    n, st_hbm, in_hbm, gy_hbm, dec_hbm, wi_ref, wo_ref,
    gi_ref, gik_ref, gok_ref, gd_ref,
    wout, win, stt, int_, eg, ea, em, og, ig,
    hg_r, ha_s, ha_r, dall, last_r, pf_s, pf_r,
    ocs, ocr, oxs, oxr, ozs, ozr, ics, icr, ixs, ixr, izs, izr,
    gd_s, gd_r, st_ref, in_ref, gy_ref, dec_ref, ss, rs, ls,
):
    f32, bf16 = jnp.float32, jnp.bfloat16
    frames, chans = dec_ref.shape
    n_cells, units = in_ref.shape
    cells = n_cells // frames
    n_cols = cells // 2
    nz = n // 2
    tm, c = lax.axis_index("tm"), lax.axis_index("rows")
    g = lax.axis_index("groups")
    z, x = tm // 2, lax.rem(tm, 2)
    counter = [0]

    def fresh(count):
        first = counter[0]
        counter[0] += count
        return first

    def remote(src, dst, i, t, r, away=None):
        return pltpu.make_async_remote_copy(
            src_ref=src, dst_ref=dst, send_sem=ss.at[i], recv_sem=rs.at[i],
            device_id={"groups": g if away is None else away, "tm": t, "rows": r},
            device_id_type=pl.DeviceIdType.MESH,
        )

    local = [
        pltpu.make_async_copy(src, dst, ls.at[i])
        for i, (src, dst) in enumerate(
            ((gy_hbm, gy_ref), (st_hbm, st_ref), (in_hbm, in_ref), (dec_hbm, dec_ref))
        )
    ]
    for copy in local:
        copy.start()

    def wrap(value, size):
        return lax.rem(value + size, size)

    sends = []

    def start(*what):
        copy = remote(*what)
        copy.start()
        sends.append(copy)
        return copy

    barrier = pltpu.get_barrier_semaphore()
    me = tm * 2 + c

    def greet(step, carry):
        other = lax.rem(me + step, 2 * n)
        pl.semaphore_signal(
            barrier, inc=1, device_id={"tm": other // 2, "rows": lax.rem(other, 2)},
            device_id_type=pl.DeviceIdType.MESH,
        )
        return carry

    lax.fori_loop(1, 2 * n, greet, 0)
    pl.semaphore_signal(
        barrier, inc=1, device_id={"groups": 1 - g, "tm": tm, "rows": c},
        device_id_type=pl.DeviceIdType.MESH,
    )
    pl.semaphore_wait(barrier, 2 * n)

    class Gather:
        def __init__(self, own, full, own_sem, by_rows):
            self.own, self.full, self.rows = own, full, own.shape[0]
            self.base, self.by_rows = fresh(6 * nz), by_rows
            self.place = pltpu.make_async_copy(own, self.slot(z, x, c), ls.at[own_sem])

        def slot(self, zz, xx, cc):
            return self.full.at[pl.ds(((zz * 2 + xx) * 2 + cc) * self.rows, self.rows)]

        def part(self, ref):
            if self.by_rows:
                third = self.rows // 3
                return ref.at[pl.ds(g * third, 2 * third)]
            half = self.full.shape[1] // 2
            return ref.at[:, pl.ds(pl.multiple_of(g * half, half), half)]

        def rest(self, ref):
            if self.by_rows:
                third = self.rows // 3
                return ref.at[pl.ds(2 * g * third, third)]
            return self.part(ref)

        def y_send(self, block, i):
            rest = self.rest(block)
            self.y_copies.append(start(rest, rest, self.base + 2 * nz + i, tm, c, 1 - g))

        def x_send(self, src, block, i):
            self.x_copies.append(
                start(self.part(src), self.part(block), self.base + nz + i, z * 2 + 1 - x, c)
            )

        def begin(self):
            mine = self.slot(z, x, c)
            self.place.start()
            self.x_copies, self.y_copies, self.c_copies = [], [], []
            self.z_copies = [
                start(
                    self.part(self.own), self.part(mine), self.base + o,
                    wrap(z + o, nz) * 2 + x, c,
                )
                for o in range(1, nz)
            ]
            self.x_send(self.own, mine, 0)
            self.c_copies = [start(self.own, mine, self.base + 4 * nz, tm, 1 - c)]

        def after_z(self):
            for o in range(1, nz):
                self.z_copies[o - 1].wait_recv()
                block = self.slot(wrap(z - o, nz), x, c)
                self.y_send(block, o)
                self.x_send(block, block, o)

        def after_x(self):
            for o in range(nz):
                self.x_copies[o].wait_recv()
                self.y_send(self.slot(wrap(z - o, nz), 1 - x, c), nz + o)

        def after_y(self):
            for i in range(1, 2 * nz):
                self.y_copies[i - 1].wait_recv()
                block = self.slot(wrap(z - i % nz, nz), x if i < nz else 1 - x, c)
                self.c_copies.append(start(block, block, self.base + 4 * nz + i, tm, 1 - c))

        def finish(self):
            for copy in self.c_copies:
                copy.wait_recv()
            self.place.wait()

    class Scatter:
        def __init__(self, acc, out, cs, cr, xs, xr, zs, zr):
            self.acc, self.out, self.rows = acc, out, out.shape[0]
            self.cs, self.cr, self.xs, self.xr, self.zs, self.zr = cs, cr, xs, xr, zs, zr
            self.base, self.c_copies = fresh(2 * nz + 1), []
            self.z_copies = []

        def part(self, t, cc):
            return self.acc[pl.ds((t * 2 + cc) * self.rows, self.rows), :]

        def core(self, low, high):
            def pack(t, carry):
                self.cs[t] = self.part(t, 1 - c).astype(bf16)
                return carry

            lax.fori_loop(low, high, pack, 0)
            span = pl.ds(low, high - low)
            i = self.base + (2 * nz if low else 0)
            self.c_copies.append(start(self.cs.at[span], self.cr.at[span], i, tm, 1 - c))

        def across(self):
            for copy in self.c_copies:
                copy.wait_recv()
            self.x_copies = []
            for o in range(1, nz + 1):
                t = wrap(z + o, nz) * 2 + 1 - x
                self.xs[o - 1] = (self.part(t, c) + self.cr[t].astype(f32)).astype(bf16)
                self.x_copies.append(
                    start(
                        self.xs.at[o - 1], self.xr.at[o - 1], self.base + o, z * 2 + 1 - x, c
                    )
                )

        def total(self, o):
            t = wrap(z + o, nz) * 2 + x
            return self.part(t, c) + self.cr[t].astype(f32) + self.xr[o - 1].astype(f32)

        def along(self):
            for o in range(1, nz):
                self.along_one(o)
            self.settle()

        def along_one(self, o):
            self.x_copies[o - 1].wait_recv()
            self.zs[o - 1] = self.total(o).astype(bf16)
            self.z_copies.append(
                start(
                    self.zs.at[o - 1], self.zr.at[o - 1], self.base + nz + o,
                    wrap(z + o, nz) * 2 + x, c,
                )
            )

        def settle(self):
            self.x_copies[nz - 1].wait_recv()
            self.out[...] = self.total(nz)

        def finish(self):
            for o in range(1, nz):
                self.z_copies[o - 1].wait_recv()
                self.out[...] += self.zr[o - 1].astype(f32)

    gather_out = Gather(wo_ref, wout, 4, False)
    gather_in = Gather(wi_ref, win, 5, False)
    halo_sem = fresh(frames)
    halo = []
    for t in range(frames):
        row = gy_hbm.at[pl.ds(t * cells + (1 - c) * n_cols, n_cols)]
        halo.append(start(row, hg_r.at[t], halo_sem + t, tm, 1 - c))
    gather_out.begin()
    dec_sem = fresh(n)
    dec_copies = [
        start(dec_hbm, dall.at[tm], dec_sem + o, wrap(tm + o, n), c) for o in range(1, n)
    ]
    last_copy = start(
        st_hbm.at[pl.ds((frames - 1) * cells, cells)], last_r, fresh(1), wrap(tm + 1, n), c
    )

    def spread(ext, received, width):
        def one(t, carry):
            ext[1, t, 3 * (1 - c)] = received[t]
            ext[1, t, 3 * c] = jnp.zeros((n_cols, width), bf16)
            field = ext[1, t].astype(f32).reshape(4 * n_cols, width)
            col = lax.rem(
                lax.broadcasted_iota(jnp.int32, (4 * n_cols, width), 0), n_cols
            )
            up = jnp.where(col == 0, 0.0, pltpu.roll(field, 1, 0))
            down = jnp.where(col == n_cols - 1, 0.0, pltpu.roll(field, 4 * n_cols - 1, 0))
            ext[2, t] = up.astype(bf16).reshape(4, n_cols, width)
            ext[0, t] = down.astype(bf16).reshape(4, n_cols, width)
            return carry

        lax.fori_loop(0, frames, one, 0)

    def tap(ext, k, width):
        return ext[lax.rem(k, 3), :, pl.ds(2 - k // 3, 2)].reshape(n_cells, width)

    def last_with_last(a, b):
        return lax.dot_general(a, b, (((1,), (1,)), ((), ())), preferred_element_type=f32)

    for copy in local:
        copy.wait()
    dall[tm] = dec_ref[...]
    stt[...] = st_ref[...].T
    int_[...] = in_ref[...].T
    for copy in halo:
        copy.wait_recv()
    for t in range(frames):
        eg[1, t, 1:3] = gy_ref[pl.ds(t * cells, cells), :].reshape(2, n_cols, units)
    spread(eg, hg_r, units)
    gather_out.after_z()
    gather_in.begin()

    def out_tap(k, carry):
        og[pl.ds(pl.multiple_of(k * chans, chans), chans), :] = jnp.dot(
            stt[...], tap(eg, k, units), preferred_element_type=f32
        )
        return carry

    lax.fori_loop(0, 5, out_tap, 0)
    scatter_out = Scatter(og, gok_ref, ocs, ocr, oxs, oxr, ozs, ozr)
    scatter_in = Scatter(ig, gik_ref, ics, icr, ixs, ixr, izs, izr)
    scatter_out.core(0, n // 2)
    lax.fori_loop(5, 9, out_tap, 0)
    scatter_out.core(n // 2, n)
    gather_out.after_x()
    scatter_out.across()
    em[...] = jnp.zeros_like(em)
    gather_out.after_y()
    gather_out.finish()

    def emit_tap(k, carry):
        em[...] += last_with_last(
            tap(eg, k, units), wout[pl.ds(pl.multiple_of(k * chans, chans), chans), :]
        )
        return carry

    lax.fori_loop(0, 9, emit_tap, 0)

    carried = jnp.zeros((cells, chans), f32)
    for t in range(frames - 1, -1, -1):
        here = em[pl.ds(t * cells, cells), :] + carried
        em[pl.ds(t * cells, cells), :] = here
        carried = dec_ref[pl.ds(t, 1), :] * here

    for copy in dec_copies:
        copy.wait_recv()

    def block_decay(steps):
        block = dall[wrap(tm + steps, n)]
        value = block[0:1]
        for t in range(1, frames):
            value = value * block[t : t + 1]
        return value

    pf_s[0] = carried.astype(bf16)
    reach, slot, total, first = 1, 0, None, True
    while True:
        offsets = [1, 2, 3] if first else [reach, 2 * reach]
        sems = fresh(len(offsets))
        copies = [
            start(pf_s.at[slot], pf_r.at[len_], sems + j, wrap(tm - d, n), c)
            for j, (d, len_) in enumerate(
                (d, (0 if first else 3) + j) for j, d in enumerate(offsets)
            )
        ]
        weight, at = None, 1
        for j, d in enumerate(offsets):
            copies[j].wait_recv()
            while at < d + (0 if first else 1):
                factor = block_decay(at)
                weight = factor if weight is None else weight * factor
                at += 1
            item = pf_r[(0 if first else 3) + j].astype(f32)
            if weight is not None:
                item = weight * item
            item = jnp.where(tm + d < n, item, 0.0)
            total = item if total is None else total + item
        reach = 3 if first else 3 * reach
        if reach >= n - 1:
            break
        first = False
        slot += 1
        pf_s[slot] = total.astype(bf16)
    em_in = total

    factor = None
    for t in range(frames - 1, -1, -1):
        add = em_in
        if factor is not None:
            add = factor * add
        here = em[pl.ds(t * cells, cells), :] + add
        em[pl.ds(t * cells, cells), :] = here
        rounded = here.astype(bf16).reshape(2, n_cols, chans)
        ea[1, t, 1:3] = rounded
        row = dec_ref[pl.ds(t, 1), :]
        factor = row if factor is None else factor * row

    def edge(t, carry):
        ha_s[t] = ea[1, t, 2 - c]
        return carry

    lax.fori_loop(0, frames, edge, 0)
    adj_copy = start(ha_s, ha_r, fresh(1), tm, 1 - c)

    gather_in.after_z()
    last_copy.wait_recv()
    for t in range(frames):
        if t == 0:
            before = jnp.where(tm > 0, last_r[...].astype(f32), 0.0)
        else:
            before = st_ref[pl.ds((t - 1) * cells, cells), :].astype(f32)
        gd_s[pl.ds(t, 1), :] = jnp.sum(
            em[pl.ds(t * cells, cells), :] * before, axis=0, keepdims=True
        )
    gd_copy = start(gd_s, gd_r, fresh(1), tm, 1 - c)

    scatter_out.along()
    adj_copy.wait_recv()
    spread(ea, ha_r, chans)

    def in_tap(k, carry):
        ig[pl.ds(pl.multiple_of(k * units, units), units), :] = jnp.dot(
            int_[...], tap(ea, k, chans), preferred_element_type=f32
        )
        return carry

    lax.fori_loop(0, 5, in_tap, 0)
    scatter_in.core(0, n // 2)
    lax.fori_loop(5, 9, in_tap, 0)
    scatter_in.core(n // 2, n)
    gather_in.after_x()
    scatter_in.across()
    gather_in.after_y()
    gather_in.finish()
    em[:, :units] = jnp.zeros((n_cells, units), f32)

    def back_tap(k, carry):
        em[:, :units] += last_with_last(
            tap(ea, k, chans), win[pl.ds(pl.multiple_of(k * units, units), units), :]
        )
        return carry

    for o in range(1, nz):
        lax.fori_loop(9 * (o - 1) // (nz - 1), 9 * o // (nz - 1), back_tap, 0)
        scatter_in.along_one(o)
    scatter_in.settle()
    gi_ref[...] = em[:, :units].astype(bf16)
    gd_copy.wait_recv()
    gd_ref[...] = gd_s[...] + gd_r[...]
    scatter_out.finish()
    scatter_in.finish()
    for copy in sends:
        copy.wait_send()


def fused_body(states, inputs, grad_y, decay, in_kernel, out_kernel):
    frames, band, n_cols, chans = states.shape
    units = inputs.shape[3]
    n = lax.axis_size("tm")
    nz = n // 2
    cells = band * n_cols
    n_cells = frames * cells
    ri, ro = in_kernel.shape[0], out_kernel.shape[0]
    f32, bf16 = jnp.float32, jnp.bfloat16
    V = pltpu.VMEM
    n_sems = 128
    outs = pl.pallas_call(
        functools.partial(ring_kernel, n),
        out_shape=(
            jax.ShapeDtypeStruct((n_cells, units), bf16),
            jax.ShapeDtypeStruct((ri, chans), f32),
            jax.ShapeDtypeStruct((ro, units), f32),
            jax.ShapeDtypeStruct((frames, chans), f32),
        ),
        in_specs=[pl.BlockSpec(memory_space=pltpu.HBM)] * 6,
        out_specs=tuple([pl.BlockSpec(memory_space=pltpu.VMEM)] * 4),
        scratch_shapes=[
            V((9 * chans, units), bf16),
            V((9 * units, chans), bf16),
            V((chans, n_cells), bf16),
            V((units, n_cells), bf16),
            V((3, frames, 4, n_cols, units), bf16),
            V((3, frames, 4, n_cols, chans), bf16),
            V((n_cells, chans), f32),
            V((9 * chans, units), f32),
            V((9 * units, chans), f32),
            V((frames, n_cols, units), bf16),
            V((frames, n_cols, chans), bf16),
            V((frames, n_cols, chans), bf16),
            V((n, frames, chans), f32),
            V((cells, chans), bf16),
            V((2, cells, chans), bf16),
            V((5, cells, chans), bf16),
        ]
        + [
            V(shape, bf16)
            for r, w in ((ro, units), (ri, chans))
            for shape in (
                (n, r, w), (n, r, w), (nz, r, w), (nz, r, w), (nz - 1, r, w), (nz - 1, r, w),
            )
        ]
        + [
            V((frames, chans), f32),
            V((frames, chans), f32),
            V((n_cells, chans), bf16),
            V((n_cells, units), bf16),
            V((n_cells, units), bf16),
            V((frames, chans), f32),
            pltpu.SemaphoreType.DMA((n_sems,)),
            pltpu.SemaphoreType.DMA((n_sems,)),
            pltpu.SemaphoreType.DMA((6,)),
        ],
        compiler_params=pltpu.CompilerParams(
            collective_id=0, has_side_effects=True, vmem_limit_bytes=60 << 20
        ),
    )(
        states.reshape(n_cells, chans),
        inputs.reshape(n_cells, units),
        grad_y.reshape(n_cells, units),
        decay,
        in_kernel,
        out_kernel,
    )
    return (outs[0].reshape(frames, band, n_cols, units),) + tuple(outs[1:])


def one_device(*arrays):
    states, in_kernel, out_kernel = arrays[0], arrays[4], arrays[5]
    n = lax.axis_size("tm")
    fits = (
        n % 2 == 0 and 4 <= n <= 10 and lax.axis_size("rows") == 2
        and states.shape[1] == 2 and states.shape[0] == 8
        and lax.axis_size("groups") == 2 and states.shape[3] % 256 == 0
        and in_kernel.shape[0] % 16 == 0 and out_kernel.shape[0] % 48 == 0
    )
    return fused_body(*arrays) if fits else body(*arrays)


def solution(mesh):
    return jax.shard_map(
        one_device,
        mesh=mesh,
        in_specs=(
            P(("groups", "tm"), "rows", None, None),
            P(("groups", "tm"), "rows", None, None),
            P(("groups", "tm"), "rows", None, None),
            P(("groups", "tm"), None),
            P(("tm", "rows"), None),
            P(("tm", "rows"), None),
        ),
        out_specs=(
            P(("groups", "tm"), "rows", None, None),
            P(("groups", "tm", "rows"), None),
            P(("groups", "tm", "rows"), None),
            P(("groups", "tm"), None),
        ),
        check_vma=False,
    )
```
